32 devices in a mesh: seq: 8 (over z, x), chan: 2 (over y), dp: 2 (over core).
Axes of the slice: x: 2, y: 2, z: 4, core: 2. Of those that a mesh axis runs over, the one named last changes fastest.
Arguments:
- ssm_input: bfloat16 [2, 1024, 4096], P('dp', 'seq', 'chan'), may hold values from -6 to 6
- gate_z: bfloat16 [2, 1024, 4096], P('dp', 'seq', 'chan'), may hold values from -6 to 6
- b_proj: bfloat16 [2, 1024, 128], P('dp', 'seq'), may hold values from -0.52734375 to 0.52734375
- c_proj: bfloat16 [2, 1024, 128], P('dp', 'seq'), may hold values from -6 to 6
- step_size: float32 [2, 1024, 64], P('dp', 'seq', 'chan'), may hold values from 0.02 to 0.2
- log_decay: float32 [2, 1024, 64], P('dp', 'seq', 'chan'), may hold values from -1 to 0, as said below
- skip_d: float32 [64], P('chan'), may hold values from 0.5 to 1.5
- norm_gain: float32 [4096], P('chan'), may hold values from 0.5 to 1.5
- w_out: bfloat16 [4096, 2048], P('chan'), may hold values from -0.09375 to 0.09375
- d_out: bfloat16 [2, 1024, 2048], P('dp', 'seq', 'chan'), may hold values from -6 to 6
- game_lengths: int32 [2, 4], P('dp'), may hold values from 1 to 512, 1024 in all within a row
Outputs:
- out: bfloat16 [2, 1024, 2048], P('dp', 'seq', 'chan')
- grad_x: bfloat16 [2, 1024, 4096], P('dp', 'seq', 'chan')
- grad_gain: float32 [4096], P('chan')
- grad_skip: float32 [64], P('chan')
The draws below stay inside these ranges and needn't reach their ends.
Inputs may be any that keep to these rules, and one draw needn't show every extreme that they name: `game_lengths`: each row's 4 game lengths sum to 1024, and the longest is exactly 512. `log_decay`: a log decay per position and head.
All inputs are finite; a program needn't handle non-finite values.
Results may differ from the reference program's by a relative error of at most 0.017.
Values may be sent and summed in bfloat16 or wider, within the bound.
No kernel may reach another device: no remote copies, remote signals or barrier semaphores. Data moves between devices by JAX's collectives and lax.ppermute only.
A program may use at most 64 MiB of HBM per device.

```python
import math
import jax
import jax.numpy as jnp
import numpy as np
from jax import lax

D = 2048
MIXER_HEADS = 64
HEADDIM = 64
DSTATE = 128
L_DEV = 128
GAMES = 4
BLOCK = 128
SEQUENCE_LENGTH = 1024
BATCH_SEQUENCES = 2


def draw_log_decay(key, part):
    random_keys = jax.random.split(jax.random.fold_in(key, 71), 7)
    fast_share = 0.5
    fast_pick = jax.random.uniform(random_keys[0], (BATCH_SEQUENCES, 1, MIXER_HEADS), jnp.float32) < fast_share
    fast_rate = jnp.exp(jax.random.uniform(random_keys[1], (BATCH_SEQUENCES, 1, MIXER_HEADS), jnp.float32, jnp.log(0.02), jnp.log(0.035)))
    slow_rate = jnp.exp(jax.random.uniform(random_keys[2], (BATCH_SEQUENCES, 1, MIXER_HEADS), jnp.float32, jnp.log(0.1 / SEQUENCE_LENGTH), jnp.log(0.7 / SEQUENCE_LENGTH)))
    baseline_rate = jnp.where(fast_pick, fast_rate, slow_rate)
    jaggedness = jnp.exp(jax.random.uniform(random_keys[3], (BATCH_SEQUENCES, SEQUENCE_LENGTH, MIXER_HEADS), jnp.float32, -0.7, 0.7))
    worker_level = jnp.exp(jax.random.uniform(random_keys[4], (BATCH_SEQUENCES, SEQUENCE_LENGTH // L_DEV, MIXER_HEADS), jnp.float32, -0.7, 0.7))
    worker_level = jnp.repeat(worker_level, L_DEV, axis=1)
    spike_places = jax.random.randint(random_keys[5], (BATCH_SEQUENCES, 3, MIXER_HEADS), 0, SEQUENCE_LENGTH)
    spike_depth = jax.random.uniform(random_keys[6], (BATCH_SEQUENCES, 3, MIXER_HEADS), jnp.float32, jnp.log(0.5), jnp.log(0.8))
    sequence_positions = jnp.arange(SEQUENCE_LENGTH, dtype=jnp.int32)
    spike_found = sequence_positions[None, :, None, None] == spike_places[:, None, :, :]
    spike_events = jnp.sum(jnp.where(spike_found, spike_depth[:, None, :, :], 0.0), axis=2)
    total = -baseline_rate * jaggedness * worker_level + spike_events
    return jnp.maximum(total, -1.0).astype(jnp.float32)


def shard_levels(key, dims, cuts, low, high):
    level = 1.0
    for dim, parts in cuts:
        draws = jax.random.uniform(jax.random.fold_in(jax.random.fold_in(key, 6), dim), (parts,), jnp.float32, low / len(cuts), high / len(cuts))
        level = level * jnp.repeat(jnp.exp(draws), dims[dim] // parts).reshape((-1,) + (1,) * (len(dims) - 1 - dim))
    return level


def profile(amount, total, reach, slope):
    loads = [(1 << 20) // math.isqrt(grade ** slope) + 1 for grade in range(2, amount + 1)]
    surplus, counts = total - reach - (amount - 1), [1] * (amount - 1)
    while surplus > 0:
        candidates = [i for i in range(amount - 1) if counts[i] < reach]
        pool, left = sum([loads[i] for i in candidates]), surplus
        for i in candidates:
            addition = min(reach - counts[i], max(1, left * loads[i] // pool), surplus)
            counts[i] = counts[i] + addition
            surplus = surplus - addition
    return np.array([reach] + counts)


def ragged(key, count, total, reach, lean):
    if count == 2:
        one = jax.random.randint(key, (), max(1, total - reach), min(reach, total - 1) + 1)
        return jnp.stack([one, total - one])
    tallies = jnp.asarray(profile(count, total, reach, lean), jnp.int32)
    twos = (count - 1) // 2
    source_of, receiver = tallies[1:1 + 2 * twos:2], tallies[2:2 + 2 * twos:2]
    slack = jnp.minimum(source_of - 1, reach - receiver)
    passed = jax.random.randint(jax.random.fold_in(key, 1), (twos,), 0, 1 << 20) % (slack + 1)
    tallies = tallies.at[1:1 + 2 * twos:2].set(source_of - passed).at[2:2 + 2 * twos:2].set(receiver + passed)
    return tallies[jax.random.permutation(jax.random.fold_in(key, 2), count)]


def normal_values(rng, extent, deviation, bound, cuts=(), kind=jnp.bfloat16):
    gain = shard_levels(rng, extent, cuts, -0.22, 0.18) if cuts else 1.0
    entries = jax.random.normal(rng, extent, jnp.float32) * deviation * gain
    return jnp.minimum(jnp.maximum(entries, -bound), bound).astype(kind)


def setup_inputs(seed: int = 0) -> dict:
    seeds = jax.random.split(jax.random.key(seed), 12)
    ssm_input = normal_values(seeds[0], (BATCH_SEQUENCES, SEQUENCE_LENGTH, MIXER_HEADS * HEADDIM), 1.0, 6.0, ((0, 2), (1, 8), (2, 2)))
    gate_z = normal_values(seeds[1], (BATCH_SEQUENCES, SEQUENCE_LENGTH, MIXER_HEADS * HEADDIM), 1.0, 6.0, ((0, 2), (1, 8), (2, 2)))
    b_proj = normal_values(seeds[2], (BATCH_SEQUENCES, SEQUENCE_LENGTH, DSTATE), (DSTATE ** -0.5), 0.52734375, ((0, 2), (1, 8)))
    c_proj = normal_values(seeds[3], (BATCH_SEQUENCES, SEQUENCE_LENGTH, DSTATE), 1.0, 6.0, ((0, 2), (1, 8)))
    step_size = jnp.clip(jnp.exp(math.log(0.2) - 2.3025851 * jax.random.uniform(seeds[4], (BATCH_SEQUENCES, SEQUENCE_LENGTH, MIXER_HEADS), jnp.float32) ** shard_levels(seeds[4], (BATCH_SEQUENCES, SEQUENCE_LENGTH, MIXER_HEADS), ((0, 2), (1, 8), (2, 2)), -0.2, 0.2)), 0.02, 0.2)
    log_decay = draw_log_decay(jax.random.fold_in(seeds[11], 71), 0)
    skip_d = jnp.clip(0.5 + 1.0 * jax.random.uniform(seeds[6], (MIXER_HEADS,), jnp.float32) ** shard_levels(seeds[6], (MIXER_HEADS,), ((0, 2),), -0.2, 0.2), 0.5, 1.5)
    norm_gain = jnp.clip(1.0 + 0.1 * jax.random.normal(seeds[7], (MIXER_HEADS * HEADDIM,), jnp.float32), 0.5, 1.5)
    w_out = normal_values(seeds[8], (MIXER_HEADS * HEADDIM, D), (MIXER_HEADS * HEADDIM) ** -0.5, 0.09375, ((0, 2),))
    d_out = normal_values(seeds[9], (BATCH_SEQUENCES, SEQUENCE_LENGTH, D), 1.0, 6.0, ((0, 2), (1, 8), (2, 2)))
    game_lengths = jax.vmap(lambda own: ragged(own, GAMES, SEQUENCE_LENGTH, SEQUENCE_LENGTH // 2, 2))(jax.random.split(seeds[10], BATCH_SEQUENCES)).reshape((BATCH_SEQUENCES, GAMES)).astype(jnp.int32)
    return dict(ssm_input=ssm_input, gate_z=gate_z, b_proj=b_proj, c_proj=c_proj, step_size=step_size, log_decay=log_decay, skip_d=skip_d, norm_gain=norm_gain, w_out=w_out, d_out=d_out, game_lengths=game_lengths)


NORM_EPS = 1e-05
PRECISE = lax.Precision.HIGHEST

def block_parts(c_block, b_block, dt_block, decay_block, reset_block):
    block_len = c_block.shape[0]
    running = jnp.cumsum(decay_block, axis=0)
    reset_count = jnp.cumsum(reset_block, axis=0).astype(jnp.int32)
    scores = jnp.dot(c_block, b_block.T, preferred_element_type=jnp.float32)
    indices = jnp.arange(block_len, dtype=jnp.int32)
    allowed = (indices[:, None] >= indices[None, :]) & (reset_count[:, None] == reset_count[None, :])
    log_gap = running.T[:, :, None] - running.T[:, None, :]
    mixing = jnp.where(allowed[None], jnp.exp(jnp.minimum(log_gap, 0.0)), 0.0) * scores[None] * dt_block.T[:, None, :]
    mixing = mixing.astype(jnp.bfloat16)
    end_count = reset_count[-1]
    carry_weight = jnp.where((reset_count == 0)[:, None], jnp.exp(running), 0.0)
    tail_weight = jnp.where((reset_count == end_count)[:, None], jnp.exp(running[-1][None, :] - running), 0.0)
    block_decay = jnp.where(end_count == 0, jnp.exp(running[-1]), 0.0)
    return (mixing, carry_weight, tail_weight, block_decay)

def one_sequence(ssm_input, gate_z, b_proj, c_proj, step_size, log_decay, starts, skip_d, norm_gain, w_out, d_out):
    sequence_positions = jnp.arange(SEQUENCE_LENGTH, dtype=jnp.int32)
    resets = jnp.any(sequence_positions[:, None] == starts[None, :], axis=1).astype(jnp.int32)
    count_blocks = SEQUENCE_LENGTH // BLOCK

    def blocked(array):
        return array.reshape((count_blocks, BLOCK) + array.shape[1:])
    x_heads = ssm_input.reshape(SEQUENCE_LENGTH, MIXER_HEADS, HEADDIM)
    zero_state = jnp.zeros((MIXER_HEADS, DSTATE, HEADDIM), jnp.float32)

    def forward_step(state, block_inputs):
        x_block, c_block, b_block, dt_block, decay_block, reset_block = block_inputs
        mixing, carry_weight, tail_weight, block_decay = block_parts(c_block, b_block, dt_block, decay_block, reset_block)
        inside = jnp.einsum('hts,shp->thp', mixing.astype(jnp.float32), x_block.astype(jnp.float32))
        carried = carry_weight[:, :, None] * jnp.einsum('tn,hnp->thp', c_block.astype(jnp.float32), state, precision=PRECISE)
        scaled = ((tail_weight * dt_block)[:, :, None] * x_block.astype(jnp.float32)).astype(jnp.bfloat16)
        fresh_state = jnp.einsum('sn,shp->hnp', b_block.astype(jnp.float32), scaled.astype(jnp.float32))
        return (block_decay[:, None, None] * state + fresh_state, inside + carried)
    _, ssd_blocks = lax.scan(forward_step, zero_state, (blocked(x_heads), blocked(c_proj), blocked(b_proj), blocked(step_size), blocked(log_decay), blocked(resets)))
    ssd_out = ssd_blocks.reshape(SEQUENCE_LENGTH, MIXER_HEADS, HEADDIM) + skip_d[None, :, None] * x_heads.astype(jnp.float32)
    gate_act = jax.nn.silu(gate_z.astype(jnp.float32))
    gated = ssd_out.reshape(SEQUENCE_LENGTH, MIXER_HEADS * HEADDIM) * gate_act
    inv_rms = lax.rsqrt(lax.optimization_barrier(jnp.mean(gated * gated, axis=1)) + NORM_EPS)
    normed = (gated * norm_gain).astype(jnp.bfloat16)
    projected = jnp.dot(normed, w_out, preferred_element_type=jnp.float32)
    out = (inv_rms[:, None] * projected).astype(jnp.bfloat16)
    pulled = jnp.dot(d_out, w_out.T, preferred_element_type=jnp.float32)
    out_dot = lax.optimization_barrier(jnp.sum(d_out.astype(jnp.float32) * projected, axis=1))
    d_normed = inv_rms[:, None] * pulled
    gain_part = lax.optimization_barrier(jnp.sum(gated * d_normed, axis=0))
    d_ssd = ((norm_gain * d_normed - (inv_rms ** 3 * out_dot / (MIXER_HEADS * HEADDIM))[:, None] * gated) * gate_act).astype(jnp.bfloat16)
    d_heads = d_ssd.reshape(SEQUENCE_LENGTH, MIXER_HEADS, HEADDIM)
    skip_part = lax.optimization_barrier(jnp.sum(d_heads.astype(jnp.float32) * x_heads.astype(jnp.float32), axis=(0, 2)))

    def backward_step(adjoint, block_inputs):
        d_block, c_block, b_block, dt_block, decay_block, reset_block = block_inputs
        mixing, carry_weight, tail_weight, block_decay = block_parts(c_block, b_block, dt_block, decay_block, reset_block)
        inside = jnp.einsum('hts,thp->shp', mixing.astype(jnp.float32), d_block.astype(jnp.float32))
        carried = (dt_block * tail_weight)[:, :, None] * jnp.einsum('sn,hnp->shp', b_block.astype(jnp.float32), adjoint, precision=PRECISE)
        weighted = (carry_weight[:, :, None] * d_block.astype(jnp.float32)).astype(jnp.bfloat16)
        fresh_adjoint = jnp.einsum('tn,thp->hnp', c_block.astype(jnp.float32), weighted.astype(jnp.float32))
        return (fresh_adjoint + block_decay[:, None, None] * adjoint, inside + carried)
    _, grad_blocks = lax.scan(backward_step, zero_state, (blocked(d_heads), blocked(c_proj), blocked(b_proj), blocked(step_size), blocked(log_decay), blocked(resets)), reverse=True)
    grad_heads = grad_blocks.reshape(SEQUENCE_LENGTH, MIXER_HEADS, HEADDIM) + skip_d[None, :, None] * d_heads.astype(jnp.float32)
    grad_x = grad_heads.astype(jnp.bfloat16).reshape(SEQUENCE_LENGTH, MIXER_HEADS * HEADDIM)
    return (out, grad_x, gain_part, skip_part)

def reference(ssm_input, gate_z, b_proj, c_proj, step_size, log_decay, skip_d, norm_gain, w_out, d_out, game_lengths):
    outs_list = []
    grads_list = []
    gain_total = jnp.zeros((MIXER_HEADS * HEADDIM,), jnp.float32)
    skip_total = jnp.zeros((MIXER_HEADS,), jnp.float32)
    for index in range(BATCH_SEQUENCES):
        lengths = game_lengths[index].astype(jnp.int32)
        starts = (jnp.cumsum(lengths) - lengths).astype(jnp.int32)
        out, grad_x, gain_part, skip_part = one_sequence(ssm_input[index], gate_z[index], b_proj[index], c_proj[index], step_size[index], log_decay[index], starts, skip_d, norm_gain, w_out, d_out[index])
        outs_list.append(out)
        grads_list.append(grad_x)
        gain_total = gain_total + gain_part
        skip_total = skip_total + skip_part
    return (jnp.stack(outs_list), jnp.stack(grads_list), gain_total, skip_total)
```

```python
import functools

import jax
import jax.numpy as jnp
from jax import lax
from jax.experimental import pallas as pl
from jax.experimental.pallas import tpu as pltpu
from jax.sharding import PartitionSpec as P

NORM_EPS = 1e-05
PRECISE = lax.Precision.HIGHEST
LANES = 128
F32 = jnp.float32
BF16 = jnp.bfloat16
VMEM = pl.BlockSpec(memory_space=pltpu.VMEM)
SMEM = pl.BlockSpec(memory_space=pltpu.SMEM)


def call(body, shapes, specs, scratch=()):
    return pl.pallas_call(
        body,
        out_shape=[jax.ShapeDtypeStruct(s, d) for s, d in shapes],
        in_specs=list(specs),
        out_specs=[VMEM] * len(shapes),
        scratch_shapes=list(scratch),
        name=body.__name__ if hasattr(body, "__name__") else body.func.__name__,
    )


def dot(a, b, da, db, precision=None):
    return lax.dot_general(
        a, b, (((da,), (db,)), ((), ())), precision=precision, preferred_element_type=F32
    )


def tile(width, index):
    return pl.ds(index * width, width)


def spread(weights, index, head_dim):
    per = LANES // head_dim
    rows = weights.shape[0]
    lane = lax.broadcasted_iota(jnp.int32, (rows, LANES), 1)
    result = jnp.broadcast_to(weights[:, index * per : index * per + 1], (rows, LANES))
    for k in range(1, per):
        column = weights[:, index * per + k : index * per + k + 1]
        result = jnp.where(lane >= k * head_dim, column, result)
    return result


def counts(lengths, offset, position):
    total = jnp.zeros(position.shape, jnp.int32)
    start = jnp.int32(0)
    for game in range(lengths.shape[1]):
        local = start - offset
        total = total + jnp.where((position >= local) & (local >= 0), 1, 0)
        start = start + lengths[0, game]
    return total


def triangle(n, upper):
    row = lax.broadcasted_iota(jnp.int32, (n, n), 0)
    col = lax.broadcasted_iota(jnp.int32, (n, n), 1)
    return jnp.where((row <= col) if upper else (row >= col), 1.0, 0.0).astype(F32)


def state_kernel(x, b, dt, decay, lengths, offset, payload, carry, tail, scaled, *, head_dim):
    n, heads = dt.shape
    width = x.shape[1]
    running = dot(triangle(n, False), decay[...], 1, 0, PRECISE)
    position = lax.broadcasted_iota(jnp.int32, (n, 1), 0)
    count = counts(lengths, offset[0], position)
    end = counts(lengths, offset[0], jnp.full((1, 1), n - 1, jnp.int32))
    last = running[n - 1 : n, :]
    carry[...] = jnp.where(count == 0, jnp.exp(running), 0.0)
    tails = jnp.where(count == end, jnp.exp(last - running), 0.0) * dt[...]
    tail[...] = tails
    for i in range(width // LANES):
        at = tile(LANES, i)
        scaled[:, at] = (spread(tails, i, head_dim) * x[:, at].astype(F32)).astype(BF16)
    payload[:, :width] = dot(b[...], scaled[...], 0, 0).astype(BF16)
    total = jnp.where(end == 0, jnp.exp(last), 0.0)
    high = total.astype(BF16).astype(F32)
    low = total - high
    row = lax.broadcasted_iota(jnp.int32, (heads, LANES), 0)
    col = lax.broadcasted_iota(jnp.int32, (heads, LANES), 1)
    extra = dot(high, jnp.where(row == col, 1.0, 0.0).astype(F32), 1, 0, PRECISE)
    extra = extra + dot(low, jnp.where(row + heads == col, 1.0, 0.0).astype(F32), 1, 0, PRECISE)
    payload[:, width:] = jnp.broadcast_to(extra, (payload.shape[0], LANES)).astype(BF16)


def mixing_kernel(x, b, c, dt, decay, lengths, offset, mixing, inside, *, head_dim):
    n, heads = dt.shape
    width = x.shape[1]
    per = LANES // head_dim
    running = dot(triangle(n, False), decay[...], 1, 0, PRECISE)
    across = dot(decay[...], triangle(n, True), 0, 0, PRECISE)
    t = lax.broadcasted_iota(jnp.int32, (n, n), 0)
    s = lax.broadcasted_iota(jnp.int32, (n, n), 1)
    same = counts(lengths, offset[0], t) == counts(lengths, offset[0], s)
    scores = jnp.where((t >= s) & same, dot(c[...], b[...], 1, 1), 0.0)
    lane = lax.broadcasted_iota(jnp.int32, (n, LANES), 1) // head_dim
    steps = dt[...]
    for i in range(width // LANES):
        at = tile(LANES, i)
        stepped = spread(steps, i, head_dim) * x[:, at].astype(F32)
        total = jnp.zeros((n, LANES), F32)
        for k in range(per):
            h = i * per + k
            gap = running[:, h : h + 1] - across[h : h + 1, :]
            mixed = (jnp.exp(jnp.minimum(gap, 0.0)) * scores).astype(BF16)
            mixing[h] = mixed
            total = total + dot(mixed, jnp.where(lane == k, stepped, 0.0).astype(BF16), 1, 0)
        inside[:, at] = total


def onward_kernel(parts, states, decays, *, heads, head_dim):
    count = parts.shape[0]
    width = states.shape[2]
    row = lax.broadcasted_iota(jnp.int32, (LANES, width), 0)
    col = lax.broadcasted_iota(jnp.int32, (LANES, width), 1) // head_dim
    pick = jnp.where((row == col) | (row == col + heads), 1.0, 0.0).astype(BF16)
    own = jnp.concatenate([parts[m, 0:1, width:] for m in range(count)], axis=0)
    spreads = dot(own, pick, 1, 0)
    decays[...] = spreads
    state = jnp.zeros(states.shape[1:], F32)
    states[0] = state.astype(BF16)
    for m in range(count - 1):
        state = spreads[m : m + 1, :] * state + parts[m, :, :width].astype(F32)
        states[m + 1] = state.astype(BF16)


def backward_kernel(parts, decays, states, sums):
    count = parts.shape[0]
    width = states.shape[2]
    state = jnp.zeros(states.shape[1:], F32)
    states[count - 1] = state.astype(BF16)
    for m in range(count - 1, 0, -1):
        state = decays[m : m + 1, :] * state + parts[m, :, :width].astype(F32)
        states[m - 1] = state.astype(BF16)
    total = parts[0, :, width:].astype(F32)
    for m in range(1, count):
        total = total + parts[m, :, width:].astype(F32)
    sums[...] = total


def gated_kernel(c, incoming, inside, carry, x, z, skip, gain, pulled, gated, normed, stats, *, head_dim):
    n, width = x.shape
    per = LANES // head_dim
    carries = carry[...]
    lane = lax.broadcasted_iota(jnp.int32, (1, LANES), 1)
    squares = jnp.zeros((n, LANES), F32)
    products = jnp.zeros((n, LANES), F32)
    for i in range(width // LANES):
        at = tile(LANES, i)
        skips = jnp.full((1, LANES), skip[i * per], F32)
        for k in range(1, per):
            skips = jnp.where(lane >= k * head_dim, skip[i * per + k], skips)
        left = dot(c[...], incoming[:, at], 1, 0)
        ssd = inside[:, at] + spread(carries, i, head_dim) * left + skips * x[:, at].astype(F32)
        gate = z[:, at].astype(F32)
        value = ssd * (gate / (1.0 + jnp.exp(-gate)))
        gated[:, at] = value
        scaled = (value * gain[:, at]).astype(BF16)
        normed[:, at] = scaled
        squares = squares + value * value
        products = products + scaled.astype(F32) * pulled[:, at]
    first = jnp.sum(squares, axis=1, keepdims=True)
    second = jnp.sum(products, axis=1, keepdims=True)
    lanes = lax.broadcasted_iota(jnp.int32, (n, LANES), 1)
    both = jnp.where(lanes == 0, first, second)
    stats[...] = both.T[: stats.shape[0], :]


def cotangent_kernel(
    stats, c, carry, x, z, gain, pulled, gated, d_ssd, payload, inverse, weighted, sums, *, head_dim, total, rows
):
    n, width = x.shape
    folded = jnp.concatenate([stats[...]] * (LANES // stats.shape[0]), axis=0).T
    inv = lax.rsqrt(folded[:, 0:1] / total + NORM_EPS)
    inverse[...] = inv
    factor = inv * inv * inv * folded[:, 1:2] / total
    carries = carry[...]
    tiles = width // LANES
    for i in range(tiles):
        at = tile(LANES, i)
        gate = z[:, at].astype(F32)
        act = gate / (1.0 + jnp.exp(-gate))
        value = gated[:, at]
        d_normed = inv * pulled[:, at]
        d_own = ((gain[:, at] * d_normed - factor * value) * act).astype(BF16)
        d_ssd[:, at] = d_own
        d_wide = d_own.astype(F32)
        weighted[:, at] = (spread(carries, i, head_dim) * d_wide).astype(BF16)
        sums[i : i + 1, :LANES] = jnp.sum(value * d_normed, axis=0, keepdims=True)
        sums[i : i + 1, LANES:] = jnp.sum(d_wide * x[:, at].astype(F32), axis=0, keepdims=True)
    payload[:, :width] = dot(c[...], weighted[...], 0, 0).astype(BF16)
    pieces = sums[...].astype(BF16)
    for j in range(payload.shape[0] // rows):
        payload[j * rows : (j + 1) * rows, width:] = pieces


def inside_kernel(mixing, d_ssd, dt, skip, inside, *, head_dim):
    n, width = d_ssd.shape
    per = LANES // head_dim
    steps = dt[...]
    lane = lax.broadcasted_iota(jnp.int32, (n, LANES), 1)
    for i in range(width // LANES):
        at = tile(LANES, i)
        d_own = d_ssd[:, at]
        skips = jnp.full((n, LANES), skip[i * per], F32)
        total = dot(mixing[i * per], d_own, 0, 0)
        for k in range(1, per):
            skips = jnp.where(lane >= k * head_dim, skip[i * per + k], skips)
            total = jnp.where(lane >= k * head_dim, dot(mixing[i * per + k], d_own, 0, 0), total)
        inside[:, at] = spread(steps, i, head_dim) * total + skips * d_own.astype(F32)


def input_kernel(b, incoming, inside, tail, grad, *, head_dim):
    width = inside.shape[1]
    tails = tail[...]
    for i in range(width // LANES):
        at = tile(LANES, i)
        right = dot(b[...], incoming[:, at], 1, 0)
        grad[:, at] = (inside[:, at] + spread(tails, i, head_dim) * right).astype(BF16)


def swap(value, axis):
    return lax.ppermute(value, axis, [(0, 1), (1, 0)])


def local(x, z, b, c, dt, decay, skip, gain, w_out, d_out, lengths):
    x, z, b, c, dt, decay, d_own = x[0], z[0], b[0], c[0], dt[0], decay[0], d_out[0]
    n, width = x.shape
    heads = dt.shape[1]
    head_dim = width // heads
    state_dim = b.shape[1]
    parts = lax.axis_size("seq")
    chans = lax.axis_size("chan")
    chan = lax.axis_index("chan")
    rows = state_dim // parts
    total = width * chans
    gain_row = gain[None, :]
    offset = (lax.axis_index("seq") * n).astype(jnp.int32)[None]

    if chans == 2:
        d_other = swap(d_own, "chan")
        first = chan == 0
        cotangent = jnp.concatenate(
            [jnp.where(first, d_own, d_other), jnp.where(first, d_other, d_own)], axis=1
        )
    else:
        cotangent = lax.all_gather(d_own, "chan", axis=1, tiled=True)

    payload, carry, tail = call(
        functools.partial(state_kernel, head_dim=head_dim),
        [((state_dim, width + LANES), BF16), ((n, heads), F32), ((n, heads), F32)],
        [VMEM] * 4 + [SMEM] * 2,
        [pltpu.VMEM((n, width), BF16)],
    )(x, b, dt, decay, lengths, offset)
    received = lax.all_to_all(
        payload.reshape(parts, rows, width + LANES), "seq", 0, 0, tiled=True
    )
    mixing, inside = call(
        functools.partial(mixing_kernel, head_dim=head_dim),
        [((heads, n, n), BF16), ((n, width), F32)],
        [VMEM] * 5 + [SMEM] * 2,
    )(x, b, c, dt, decay, lengths, offset)
    pulled = lax.dot_general(
        cotangent, w_out, (((1,), (1,)), ((), ())), preferred_element_type=F32
    )
    states, decays = call(
        functools.partial(onward_kernel, heads=heads, head_dim=head_dim),
        [((parts, rows, width), BF16), ((parts, width), F32)],
        [VMEM],
    )(received)
    incoming = lax.all_to_all(states, "seq", 0, 0, tiled=True).reshape(state_dim, width)
    gated, normed, stats = call(
        functools.partial(gated_kernel, head_dim=head_dim),
        [((n, width), F32), ((n, width), BF16), ((8, n), F32)],
        [VMEM] * 6 + [SMEM] + [VMEM] * 2,
    )(c, incoming, inside, carry, x, z, skip, gain_row, pulled)
    stats = stats + swap(stats, "chan") if chans == 2 else lax.psum(stats, "chan")
    d_ssd, payload, inverse = call(
        functools.partial(cotangent_kernel, head_dim=head_dim, total=total, rows=rows),
        [((n, width), BF16), ((state_dim, width + 2 * LANES), BF16), ((n, 1), F32)],
        [VMEM] * 8,
        [pltpu.VMEM((n, width), BF16), pltpu.VMEM((rows, 2 * LANES), F32)],
    )(stats, c, carry, x, z, gain_row, pulled, gated)
    received = lax.all_to_all(
        payload.reshape(parts, rows, width + 2 * LANES), "seq", 0, 0, tiled=True
    )
    grad_inside = call(
        functools.partial(inside_kernel, head_dim=head_dim),
        [((n, width), F32)],
        [VMEM] * 3 + [SMEM],
    )(mixing, d_ssd, dt, skip)[0]
    states, sums = call(
        backward_kernel,
        [((parts, rows, width), BF16), ((rows, 2 * LANES), F32)],
        [VMEM] * 2,
    )(received, decays)
    incoming = lax.all_to_all(states, "seq", 0, 0, tiled=True).reshape(state_dim, width)
    sums = sums + swap(sums, "dp") if lax.axis_size("dp") == 2 else lax.psum(sums, "dp")
    projected = jnp.dot(normed, w_out, preferred_element_type=F32)
    if chans == 2:
        half = projected.shape[1] // 2
        low, high = projected[:, :half], projected[:, half:]
        theirs = swap(jnp.where(chan == 0, high, low).astype(BF16), "chan")
        projected = jnp.where(chan == 0, low, high) + theirs.astype(F32)
    else:
        projected = lax.psum_scatter(
            projected.astype(BF16), "chan", scatter_dimension=1, tiled=True
        ).astype(F32)
    out = (inverse * projected).astype(BF16)[None]
    grad_x = call(
        functools.partial(input_kernel, head_dim=head_dim),
        [((n, width), BF16)],
        [VMEM] * 4,
    )(b, incoming, grad_inside, tail)[0][None]
    grad_gain = sums[:, :LANES].reshape(-1)
    grad_skip = jnp.sum(sums[:, LANES:].reshape(heads, head_dim), axis=1)
    return (out, grad_x, grad_gain, grad_skip)


def solution(mesh):
    return jax.shard_map(
        local,
        mesh=mesh,
        in_specs=(
            P("dp", "seq", "chan"),
            P("dp", "seq", "chan"),
            P("dp", "seq", None),
            P("dp", "seq", None),
            P("dp", "seq", "chan"),
            P("dp", "seq", "chan"),
            P("chan"),
            P("chan"),
            P("chan", None),
            P("dp", "seq", "chan"),
            P("dp", None),
        ),
        out_specs=(P("dp", "seq", "chan"), P("dp", "seq", "chan"), P("chan"), P("chan")),
        check_vma=False,
    )
```

```python
import functools

import jax
import jax.numpy as jnp
from jax import lax
from jax.experimental import pallas as pl
from jax.experimental.pallas import tpu as pltpu
from jax.sharding import PartitionSpec as P

NORM_EPS = 1e-05
PRECISE = lax.Precision.HIGHEST
LANES = 128
F32 = jnp.float32
BF16 = jnp.bfloat16
VMEM = pl.BlockSpec(memory_space=pltpu.VMEM)
SMEM = pl.BlockSpec(memory_space=pltpu.SMEM)


def call(body, shapes, specs, scratch=()):
    return pl.pallas_call(
        body,
        out_shape=[jax.ShapeDtypeStruct(s, d) for s, d in shapes],
        in_specs=list(specs),
        out_specs=[VMEM] * len(shapes),
        scratch_shapes=list(scratch),
        name=body.__name__ if hasattr(body, "__name__") else body.func.__name__,
    )


def dot(a, b, da, db, precision=None):
    return lax.dot_general(
        a, b, (((da,), (db,)), ((), ())), precision=precision, preferred_element_type=F32
    )


def tile(width, index):
    return pl.ds(index * width, width)


def spread(weights, index, head_dim):
    per = LANES // head_dim
    rows = weights.shape[0]
    lane = lax.broadcasted_iota(jnp.int32, (rows, LANES), 1)
    result = jnp.broadcast_to(weights[:, index * per : index * per + 1], (rows, LANES))
    for k in range(1, per):
        column = weights[:, index * per + k : index * per + k + 1]
        result = jnp.where(lane >= k * head_dim, column, result)
    return result


def counts(lengths, offset, position):
    total = jnp.zeros(position.shape, jnp.int32)
    start = jnp.int32(0)
    for game in range(lengths.shape[1]):
        local = start - offset
        total = total + jnp.where((position >= local) & (local >= 0), 1, 0)
        start = start + lengths[0, game]
    return total


def turned(rows):
    heads, n = rows.shape
    return jnp.concatenate([rows] * (n // heads), axis=0).T[:, :heads]


def triangle(n, upper):
    row = lax.broadcasted_iota(jnp.int32, (n, n), 0)
    col = lax.broadcasted_iota(jnp.int32, (n, n), 1)
    return jnp.where((row <= col) if upper else (row >= col), 1.0, 0.0).astype(F32)


def state_kernel(x, b, dt, decay, lengths, offset, payload, carry, tail, scaled, *, head_dim):
    heads, n = dt.shape
    width = x.shape[1]
    running = dot(triangle(n, False), decay[...], 1, 1, PRECISE)
    position = lax.broadcasted_iota(jnp.int32, (n, 1), 0)
    count = counts(lengths, offset[0], position)
    end = counts(lengths, offset[0], jnp.full((1, 1), n - 1, jnp.int32))
    last = running[n - 1 : n, :]
    carry[...] = jnp.where(count == 0, jnp.exp(running), 0.0)
    tails = jnp.where(count == end, jnp.exp(last - running), 0.0) * turned(dt[...])
    tail[...] = tails
    for i in range(width // LANES):
        at = tile(LANES, i)
        scaled[:, at] = (spread(tails, i, head_dim) * x[:, at].astype(F32)).astype(BF16)
    payload[:, :width] = dot(b[...], scaled[...], 0, 0).astype(BF16)
    total = jnp.where(end == 0, jnp.exp(last), 0.0)
    high = total.astype(BF16).astype(F32)
    low = total - high
    row = lax.broadcasted_iota(jnp.int32, (heads, LANES), 0)
    col = lax.broadcasted_iota(jnp.int32, (heads, LANES), 1)
    extra = dot(high, jnp.where(row == col, 1.0, 0.0).astype(F32), 1, 0, PRECISE)
    extra = extra + dot(low, jnp.where(row + heads == col, 1.0, 0.0).astype(F32), 1, 0, PRECISE)
    payload[:, width:] = jnp.broadcast_to(extra, (payload.shape[0], LANES)).astype(BF16)


def mixing_kernel(x, b, c, dt, decay, lengths, offset, mixing, inside, *, head_dim):
    heads, n = dt.shape
    width = x.shape[1]
    per = LANES // head_dim
    running = dot(triangle(n, False), decay[...], 1, 1, PRECISE)
    across = dot(decay[...], triangle(n, True), 1, 0, PRECISE)
    t = lax.broadcasted_iota(jnp.int32, (n, n), 0)
    s = lax.broadcasted_iota(jnp.int32, (n, n), 1)
    same = counts(lengths, offset[0], t) == counts(lengths, offset[0], s)
    scores = jnp.where((t >= s) & same, dot(c[...], b[...], 1, 1), 0.0)
    lane = lax.broadcasted_iota(jnp.int32, (n, LANES), 1) // head_dim
    steps = turned(dt[...])
    for i in range(width // LANES):
        at = tile(LANES, i)
        stepped = spread(steps, i, head_dim) * x[:, at].astype(F32)
        total = jnp.zeros((n, LANES), F32)
        for k in range(per):
            h = i * per + k
            gap = running[:, h : h + 1] - across[h : h + 1, :]
            mixed = (jnp.exp(jnp.minimum(gap, 0.0)) * scores).astype(BF16)
            mixing[h] = mixed
            total = total + dot(mixed, jnp.where(lane == k, stepped, 0.0).astype(BF16), 1, 0)
        inside[:, at] = total


def onward_kernel(parts, states, decays, *, heads, head_dim):
    count = parts.shape[0]
    width = states.shape[2]
    row = lax.broadcasted_iota(jnp.int32, (LANES, width), 0)
    col = lax.broadcasted_iota(jnp.int32, (LANES, width), 1) // head_dim
    pick = jnp.where((row == col) | (row == col + heads), 1.0, 0.0).astype(BF16)
    own = jnp.concatenate([parts[m, 0:1, width:] for m in range(count)], axis=0)
    spreads = dot(own, pick, 1, 0)
    decays[...] = spreads
    state = jnp.zeros(states.shape[1:], F32)
    states[0] = state.astype(BF16)
    for m in range(count - 1):
        state = spreads[m : m + 1, :] * state + parts[m, :, :width].astype(F32)
        states[m + 1] = state.astype(BF16)


def backward_kernel(parts, decays, states, sums):
    count = parts.shape[0]
    width = states.shape[2]
    state = jnp.zeros(states.shape[1:], F32)
    states[count - 1] = state.astype(BF16)
    for m in range(count - 1, 0, -1):
        state = decays[m : m + 1, :] * state + parts[m, :, :width].astype(F32)
        states[m - 1] = state.astype(BF16)
    total = parts[0, :, width:].astype(F32)
    for m in range(1, count):
        total = total + parts[m, :, width:].astype(F32)
    sums[...] = total


def gated_kernel(c, incoming, inside, carry, x, z, skip, gain, pulled, gated, normed, stats, *, head_dim):
    n, width = x.shape
    per = LANES // head_dim
    carries = carry[...]
    lane = lax.broadcasted_iota(jnp.int32, (1, LANES), 1)
    squares = jnp.zeros((n, LANES), F32)
    products = jnp.zeros((n, LANES), F32)
    for i in range(width // LANES):
        at = tile(LANES, i)
        skips = jnp.full((1, LANES), skip[i * per], F32)
        for k in range(1, per):
            skips = jnp.where(lane >= k * head_dim, skip[i * per + k], skips)
        left = dot(c[...], incoming[:, at], 1, 0)
        ssd = inside[:, at] + spread(carries, i, head_dim) * left + skips * x[:, at].astype(F32)
        gate = z[:, at].astype(F32)
        value = ssd * (gate / (1.0 + jnp.exp(-gate)))
        gated[:, at] = value
        scaled = (value * gain[:, at]).astype(BF16)
        normed[:, at] = scaled
        squares = squares + value * value
        products = products + scaled.astype(F32) * pulled[:, at]
    first = jnp.sum(squares, axis=1, keepdims=True)
    second = jnp.sum(products, axis=1, keepdims=True)
    lanes = lax.broadcasted_iota(jnp.int32, (n, LANES), 1)
    both = jnp.where(lanes == 0, first, second)
    stats[...] = both.T[: stats.shape[0], :]


def cotangent_kernel(
    stats, c, carry, x, z, gain, pulled, gated, d_ssd, payload, inverse, weighted, sums, *, head_dim, total, rows
):
    n, width = x.shape
    folded = jnp.concatenate([stats[...]] * (LANES // stats.shape[0]), axis=0).T
    inv = lax.rsqrt(folded[:, 0:1] / total + NORM_EPS)
    inverse[...] = inv
    factor = inv * inv * inv * folded[:, 1:2] / total
    carries = carry[...]
    tiles = width // LANES
    for i in range(tiles):
        at = tile(LANES, i)
        gate = z[:, at].astype(F32)
        act = gate / (1.0 + jnp.exp(-gate))
        value = gated[:, at]
        d_normed = inv * pulled[:, at]
        d_own = ((gain[:, at] * d_normed - factor * value) * act).astype(BF16)
        d_ssd[:, at] = d_own
        d_wide = d_own.astype(F32)
        weighted[:, at] = (spread(carries, i, head_dim) * d_wide).astype(BF16)
        sums[i : i + 1, :LANES] = jnp.sum(value * d_normed, axis=0, keepdims=True)
        sums[i : i + 1, LANES:] = jnp.sum(d_wide * x[:, at].astype(F32), axis=0, keepdims=True)
    payload[:, :width] = dot(c[...], weighted[...], 0, 0).astype(BF16)
    pieces = sums[...].astype(BF16)
    for j in range(payload.shape[0] // rows):
        payload[j * rows : (j + 1) * rows, width:] = pieces


def inside_kernel(mixing, d_ssd, dt, skip, inside, *, head_dim):
    n, width = d_ssd.shape
    per = LANES // head_dim
    steps = turned(dt[...])
    lane = lax.broadcasted_iota(jnp.int32, (n, LANES), 1)
    for i in range(width // LANES):
        at = tile(LANES, i)
        d_own = d_ssd[:, at]
        skips = jnp.full((n, LANES), skip[i * per], F32)
        total = dot(mixing[i * per], d_own, 0, 0)
        for k in range(1, per):
            skips = jnp.where(lane >= k * head_dim, skip[i * per + k], skips)
            total = jnp.where(lane >= k * head_dim, dot(mixing[i * per + k], d_own, 0, 0), total)
        inside[:, at] = spread(steps, i, head_dim) * total + skips * d_own.astype(F32)


def input_kernel(b, incoming, inside, tail, grad, *, head_dim):
    width = inside.shape[1]
    tails = tail[...]
    for i in range(width // LANES):
        at = tile(LANES, i)
        right = dot(b[...], incoming[:, at], 1, 0)
        grad[:, at] = (inside[:, at] + spread(tails, i, head_dim) * right).astype(BF16)


def swap(value, axis):
    return lax.ppermute(value, axis, [(0, 1), (1, 0)])


def local(x, z, b, c, dt, decay, skip, gain, w_out, d_out, lengths):
    x, z, b, c, dt, decay, d_own = x[0], z[0], b[0], c[0], dt[0], decay[0], d_out[0]
    n, width = x.shape
    dt, decay = dt.T, decay.T
    heads = dt.shape[0]
    head_dim = width // heads
    state_dim = b.shape[1]
    parts = lax.axis_size("seq")
    chans = lax.axis_size("chan")
    chan = lax.axis_index("chan")
    rows = state_dim // parts
    total = width * chans
    gain_row = gain[None, :]
    offset = (lax.axis_index("seq") * n).astype(jnp.int32)[None]

    if chans == 2:
        d_other = swap(d_own, "chan")
        first = chan == 0
        cotangent = jnp.concatenate(
            [jnp.where(first, d_own, d_other), jnp.where(first, d_other, d_own)], axis=1
        )
    else:
        cotangent = lax.all_gather(d_own, "chan", axis=1, tiled=True)

    payload, carry, tail = call(
        functools.partial(state_kernel, head_dim=head_dim),
        [((state_dim, width + LANES), BF16), ((n, heads), F32), ((n, heads), F32)],
        [VMEM] * 4 + [SMEM] * 2,
        [pltpu.VMEM((n, width), BF16)],
    )(x, b, dt, decay, lengths, offset)
    received = lax.all_to_all(
        payload.reshape(parts, rows, width + LANES), "seq", 0, 0, tiled=True
    )
    mixing, inside = call(
        functools.partial(mixing_kernel, head_dim=head_dim),
        [((heads, n, n), BF16), ((n, width), F32)],
        [VMEM] * 5 + [SMEM] * 2,
    )(x, b, c, dt, decay, lengths, offset)
    pulled = lax.dot_general(
        cotangent, w_out, (((1,), (1,)), ((), ())), preferred_element_type=F32
    )
    states, decays = call(
        functools.partial(onward_kernel, heads=heads, head_dim=head_dim),
        [((parts, rows, width), BF16), ((parts, width), F32)],
        [VMEM],
    )(received)
    incoming = lax.all_to_all(states, "seq", 0, 0, tiled=True).reshape(state_dim, width)
    gated, normed, stats = call(
        functools.partial(gated_kernel, head_dim=head_dim),
        [((n, width), F32), ((n, width), BF16), ((8, n), F32)],
        [VMEM] * 6 + [SMEM] + [VMEM] * 2,
    )(c, incoming, inside, carry, x, z, skip, gain_row, pulled)
    stats = stats + swap(stats, "chan") if chans == 2 else lax.psum(stats, "chan")
    d_ssd, payload, inverse = call(
        functools.partial(cotangent_kernel, head_dim=head_dim, total=total, rows=rows),
        [((n, width), BF16), ((state_dim, width + 2 * LANES), BF16), ((n, 1), F32)],
        [VMEM] * 8,
        [pltpu.VMEM((n, width), BF16), pltpu.VMEM((rows, 2 * LANES), F32)],
    )(stats, c, carry, x, z, gain_row, pulled, gated)
    received = lax.all_to_all(
        payload.reshape(parts, rows, width + 2 * LANES), "seq", 0, 0, tiled=True
    )
    grad_inside = call(
        functools.partial(inside_kernel, head_dim=head_dim),
        [((n, width), F32)],
        [VMEM] * 3 + [SMEM],
    )(mixing, d_ssd, dt, skip)[0]
    states, sums = call(
        backward_kernel,
        [((parts, rows, width), BF16), ((rows, 2 * LANES), F32)],
        [VMEM] * 2,
    )(received, decays)
    incoming = lax.all_to_all(states, "seq", 0, 0, tiled=True).reshape(state_dim, width)
    sums = sums + swap(sums, "dp") if lax.axis_size("dp") == 2 else lax.psum(sums, "dp")
    projected = jnp.dot(normed, w_out, preferred_element_type=F32)
    if chans == 2:
        half = projected.shape[1] // 2
        low, high = projected[:, :half], projected[:, half:]
        theirs = swap(jnp.where(chan == 0, high, low).astype(BF16), "chan")
        projected = jnp.where(chan == 0, low, high) + theirs.astype(F32)
    else:
        projected = lax.psum_scatter(
            projected.astype(BF16), "chan", scatter_dimension=1, tiled=True
        ).astype(F32)
    out = (inverse * projected).astype(BF16)[None]
    grad_x = call(
        functools.partial(input_kernel, head_dim=head_dim),
        [((n, width), BF16)],
        [VMEM] * 4,
    )(b, incoming, grad_inside, tail)[0][None]
    grad_gain = sums[:, :LANES].reshape(-1)
    grad_skip = jnp.sum(sums[:, LANES:].reshape(heads, head_dim), axis=1)
    return (out, grad_x, grad_gain, grad_skip)


def solution(mesh):
    return jax.shard_map(
        local,
        mesh=mesh,
        in_specs=(
            P("dp", "seq", "chan"),
            P("dp", "seq", "chan"),
            P("dp", "seq", None),
            P("dp", "seq", None),
            P("dp", "seq", "chan"),
            P("dp", "seq", "chan"),
            P("chan"),
            P("chan"),
            P("chan", None),
            P("dp", "seq", "chan"),
            P("dp", None),
        ),
        out_specs=(P("dp", "seq", "chan"), P("dp", "seq", "chan"), P("chan"), P("chan")),
        check_vma=False,
    )
```
